128 devices in a mesh: group: 8 (over y, x_lo), tensor: 16 (over x_hi, z, core).
Axes of the slice: x: 4 (x_hi: 2, x_lo: 2; x = x_hi * 2 + x_lo), y: 4, z: 4, core: 2. Of those that a mesh axis runs over, the one named last changes fastest.
Arguments:
- prefill_states: bfloat16 [32768, 8192], P('group', 'tensor'), may hold values from -6 to 6
- key_weight: bfloat16 [8192, 1024], P('tensor'), may hold values from -0.0625 to 0.0625
- value_weight: bfloat16 [8192, 1024], P('tensor'), may hold values from -0.0625 to 0.0625
- page_slot: int32 [8, 16, 32], P('group', 'tensor'), may hold values from 0 to 31, each once within a row
- decode_states: bfloat16 [32, 8192], P('group'), may hold values from -6 to 6
- query_weight: bfloat16 [8192, 8192], P(None, 'tensor'), may hold values from -0.0625 to 0.0625
- cache_keys: bfloat16 [32, 8192, 1024], P('group', 'tensor'), may hold values from -606 to 606
- cache_values: bfloat16 [32, 8192, 1024], P('group', 'tensor'), may hold values from -6 to 6
- cached_length: int32 [32], P('group'), may hold values from 1 to 8192
Outputs:
- attention_out: bfloat16 [32, 8192], P('group', 'tensor')
The draws below stay inside these ranges and needn't reach their ends.
Inputs may be any that keep to these rules, and one draw needn't show every extreme that they name: For every group g and block t, page_slot[g, t, :] is a permutation of 0 to 31.
All inputs are finite; a program needn't handle non-finite values.
Results may differ from the reference program's by a relative error of at most 0.017.
Values may be sent and summed in bfloat16 or wider, within the bound.
No kernel may reach another device: no remote copies, remote signals or barrier semaphores. Data moves between devices by JAX's collectives and lax.ppermute only.
A program may use at most 192 MiB of HBM per device.

```python
import jax
import jax.numpy as jnp
from jax import lax

D = 8192
QUERY_HEAD_COUNT = 64
KEY_VALUE_HEADS = 8
HEAD_WIDTH = 128
PAGE = 8
PRE_TOK = 4096
B_DEV = 4
KVW = 1024
QW = 8192
GROUPS = 8
RANKS = 16
PRE_ALL = 32768
DECODE_BATCH = 32
CONTEXT = 8192
PAGES_DEV = 32
PER_OWNER = 4
FRESH_ROW = 64
N_GROUP = 8
N_TENSOR = 16


def draw_cache_keys(key, part):
    normal_key = jax.random.fold_in(key, 0)
    base_draw = jnp.clip(jax.random.normal(normal_key, (DECODE_BATCH, CONTEXT, KVW), jnp.float32), -6.0, 6.0)
    return base_draw.astype(jnp.bfloat16)


def set_ends(values, key, low, top_value):
    shape = values.shape
    spot = [jax.random.randint(jax.random.fold_in(key, axis), (), 0, shape[axis]) for axis in range(len(shape))]
    values = values.at[tuple(spot)].set(low)
    longest = shape.index(max(shape))
    spot[longest] = (spot[longest] + 1) % shape[longest]
    return values.at[tuple(spot)].set(top_value)


def block_scale(rng, shape, pieces, smallest, high):
    factor_of, own = 1.0, jax.random.fold_in(rng, 6)
    for position, parts in pieces:
        heights = jnp.exp(jax.random.uniform(jax.random.fold_in(own, position), (parts,), jnp.float32, smallest / len(pieces), high / len(pieces)))
        factor_of = factor_of * jnp.repeat(heights, shape[position] // parts).reshape([-1 if axis == position else 1 for axis in range(len(shape))])
    return factor_of


def bell_draw(key, extent, width, reach, pieces=(), kind=jnp.bfloat16):
    result = jax.random.normal(key, extent, jnp.float32) * width
    if len(pieces) > 0:
        result = block_scale(key, extent, pieces, -0.22, 0.18) * result
    return jnp.clip(result, min=-reach, max=reach).astype(kind)


def setup_inputs(seed: int = 0) -> dict:
    arg_keys = jax.random.split(jax.random.key(seed), 10)
    return {
        "prefill_states": bell_draw(arg_keys[0], (PRE_ALL, D), 1.0, 6.0, ((0, 8), (1, 16))),
        "key_weight": bell_draw(arg_keys[1], (D, KVW), D ** -0.5, 0.0625, ((0, 16),)),
        "value_weight": bell_draw(arg_keys[2], (D, KVW), D ** -0.5, 0.0625, ((0, 16),)),
        "page_slot": jax.vmap(lambda own: jax.random.permutation(own, PAGES_DEV))(jax.random.split(arg_keys[3], GROUPS * RANKS)).reshape((GROUPS, RANKS, PAGES_DEV)).astype(jnp.int32),
        "decode_states": bell_draw(arg_keys[4], (DECODE_BATCH, D), 1.0, 6.0, ((0, 8),)),
        "query_weight": bell_draw(arg_keys[5], (D, QW), D ** -0.5, 0.0625, ((1, 16),)),
        "cache_keys": draw_cache_keys(jax.random.fold_in(arg_keys[9], 71), 0),
        "cache_values": bell_draw(arg_keys[7], (DECODE_BATCH, CONTEXT, KVW), 1.0, 6.0, ((0, 8), (1, 16))),
        "cached_length": set_ends(jax.random.randint(arg_keys[8], (DECODE_BATCH,), 1, CONTEXT + 1), jax.random.fold_in(arg_keys[8], 1), 1, CONTEXT).astype(jnp.int32),
    }


rope_theta = 500000.0
masked_score = -1e30


def apply_rotary(vectors, positions):
    half_width = vectors.shape[-1] // 2
    index_float = jnp.arange(half_width, dtype=jnp.float32)
    frequency = rope_theta ** (-2.0 * index_float / vectors.shape[-1])
    angles = positions[..., None].astype(jnp.float32) * frequency
    cosine_part = jnp.cos(angles)
    sine_part = jnp.sin(angles)
    first_half = vectors[..., :half_width]
    second_half = vectors[..., half_width:]
    return jnp.concatenate([first_half * cosine_part - second_half * sine_part, second_half * cosine_part + first_half * sine_part], axis=-1)


def reference(prefill_states, key_weight, value_weight, page_slot, decode_states, query_weight, cache_keys, cache_values, cached_length):
    def project(states):
        key_proj = jnp.dot(states, key_weight, preferred_element_type=jnp.float32)
        value_proj = jnp.dot(states, value_weight, preferred_element_type=jnp.float32)
        return key_proj.astype(jnp.bfloat16), value_proj.astype(jnp.bfloat16)

    fresh_keys, fresh_values = lax.map(project, prefill_states.reshape(N_GROUP, PRE_TOK, D))
    inverse = jnp.argsort(page_slot, axis=-1).astype(jnp.int32)

    def to_owners(fresh_rows):
        page_blocks = fresh_rows.reshape(N_GROUP, N_TENSOR, PAGES_DEV, PAGE * KVW)
        ordered = jnp.take_along_axis(page_blocks, inverse[..., None], axis=2)
        ordered = ordered.reshape(N_GROUP, N_TENSOR, N_GROUP, PER_OWNER * PAGE * KVW).transpose(2, 1, 0, 3)
        ordered = ordered.reshape(N_GROUP, N_TENSOR, B_DEV, FRESH_ROW, KVW).transpose(0, 2, 1, 3, 4)
        return ordered.reshape(DECODE_BATCH, N_TENSOR * FRESH_ROW, KVW)

    keys_in_place = to_owners(fresh_keys)
    owner_values = to_owners(fresh_values)
    fresh_length = N_TENSOR * FRESH_ROW
    fresh_position_index = cached_length[:, None] + jnp.arange(fresh_length, dtype=jnp.int32)[None, :]
    keys_by_owner = apply_rotary(keys_in_place.astype(jnp.float32).reshape(DECODE_BATCH, fresh_length, KEY_VALUE_HEADS, HEAD_WIDTH), fresh_position_index[:, :, None])
    keys_by_owner = keys_by_owner.reshape(DECODE_BATCH, fresh_length, KVW).astype(jnp.bfloat16)
    query_vectors = jnp.dot(decode_states, query_weight, preferred_element_type=jnp.float32).reshape(DECODE_BATCH, QUERY_HEAD_COUNT, HEAD_WIDTH)
    query_vectors = apply_rotary(query_vectors, (cached_length + fresh_length)[:, None]).astype(jnp.bfloat16).reshape(DECODE_BATCH, KEY_VALUE_HEADS, QUERY_HEAD_COUNT // KEY_VALUE_HEADS, HEAD_WIDTH)

    def attend(inputs):
        query_row, prior_keys, prior_values, incoming_keys, incoming_values, length = inputs
        key_row_block = jnp.concatenate([prior_keys, incoming_keys], axis=0).reshape(-1, KEY_VALUE_HEADS, HEAD_WIDTH).astype(jnp.float32)
        value_row_block = jnp.concatenate([prior_values, incoming_values], axis=0).reshape(-1, KEY_VALUE_HEADS, HEAD_WIDTH).astype(jnp.float32)
        scores = jnp.einsum("hgd,lhd->hgl", query_row.astype(jnp.float32), key_row_block) / (HEAD_WIDTH ** 0.5)
        usable = jnp.concatenate([jnp.arange(CONTEXT, dtype=jnp.int32) < length, jnp.ones((fresh_length,), dtype=bool)])
        scores = jnp.where(usable, scores, masked_score)
        row_peak = jnp.max(scores, axis=-1, keepdims=True)
        weights = jnp.exp(scores - row_peak)
        row_total = jnp.sum(weights, axis=-1)
        rounded = lax.optimization_barrier(weights.astype(jnp.bfloat16)).astype(jnp.float32)
        blended = jnp.einsum("hgl,lhd->hgd", rounded, value_row_block) / row_total[..., None]
        return blended.reshape(QW).astype(jnp.bfloat16)

    return lax.map(attend, (query_vectors, cache_keys, cache_values, keys_by_owner, owner_values, cached_length))
```

```python
import jax
import jax.numpy as jnp
import numpy as np
from jax import lax
from jax.experimental import pallas as pl
from jax.experimental.pallas import tpu as pltpu
from jax.sharding import PartitionSpec as P

HEAD_WIDTH = 128
PAGE = 8
BOTH = ("group", "tensor")

rope_theta = 500000.0
masked_score = -1e30

bf16 = jnp.bfloat16
f32 = jnp.float32

HALF = HEAD_WIDTH // 2
FREQUENCY = rope_theta ** (-2.0 * np.arange(HALF) / HEAD_WIDTH)
FREQUENCY_PAIR = np.concatenate([FREQUENCY, FREQUENCY]).astype(np.float32)
SIGN_PAIR = np.concatenate([-np.ones(HALF), np.ones(HALF)]).astype(np.float32)


def sent_to_all(array, axis):
    devices = lax.axis_size(axis)
    return lax.all_to_all(
        jnp.broadcast_to(array[None], (devices, *array.shape)), axis, 0, 0, tiled=True
    )


def apply_rotary(vectors, positions):
    angles = positions[..., None].astype(f32) * FREQUENCY.astype(np.float32)
    cosine_part = jnp.cos(angles)
    sine_part = jnp.sin(angles)
    first_half = vectors[..., :HALF]
    second_half = vectors[..., HALF:]
    return jnp.concatenate(
        [
            first_half * cosine_part - second_half * sine_part,
            second_half * cosine_part + first_half * sine_part,
        ],
        axis=-1,
    )


def partial_keys(states, weight, cosine, sine):
    tokens, features = states.shape
    blocks = cosine.shape[0]
    rows = tokens // blocks
    width = weight.shape[1]
    step = 2 * HEAD_WIDTH

    def kernel(x_ref, w_ref, c_ref, s_ref, o_ref):
        x = x_ref[...]
        c = c_ref[0][None]
        s = s_ref[0][None]
        for at in range(0, width, step):
            k = jnp.dot(x, w_ref[:, at : at + step], preferred_element_type=f32)
            for h in range(0, step, HEAD_WIDTH):
                part = k[:, h : h + HEAD_WIDTH].reshape(rows // PAGE, PAGE, HEAD_WIDTH)
                turned = part * c + pltpu.roll(part, HALF, 2) * s
                o_ref[:, at + h : at + h + HEAD_WIDTH] = turned.reshape(rows, HEAD_WIDTH).astype(bf16)

    return pl.pallas_call(
        kernel,
        out_shape=jax.ShapeDtypeStruct((tokens, width), bf16),
        grid=(blocks,),
        in_specs=[
            pl.BlockSpec((rows, features), lambda i: (i, 0)),
            pl.BlockSpec((features, width), lambda i: (0, 0)),
            pl.BlockSpec((1, PAGE, HEAD_WIDTH), lambda i: (i, 0, 0)),
            pl.BlockSpec((1, PAGE, HEAD_WIDTH), lambda i: (i, 0, 0)),
        ],
        out_specs=pl.BlockSpec((rows, width), lambda i: (i, 0)),
        name="partial_keys",
    )(states, weight, cosine, sine)


def gather_pages(order, pages_ref, buf, sem, row, slot, count):
    for p in range(count):
        pltpu.make_async_copy(
            pages_ref.at[order[row * count + p]], buf.at[slot, p], sem.at[slot]
        ).start()


def wait_pages(pages_ref, buf, sem, slot, count):
    pltpu.make_async_copy(pages_ref.at[pl.ds(0, count)], buf.at[slot], sem.at[slot]).wait()


def partial_scores(order, keys, queries, tables):
    tokens, width = keys.shape
    rows, heads, _ = queries.shape
    per_row = tokens // rows
    count = per_row // PAGE
    turns = tables.shape[1]
    per_turn = per_row // turns
    kv_heads = width // HEAD_WIDTH
    group = heads // kv_heads
    pages = keys.reshape(tokens // PAGE, PAGE, width)

    def kernel(order, pages_ref, q_ref, t_ref, o_ref, buf, sem):
        row = pl.program_id(0)
        slot = lax.rem(row, 2)

        @pl.when(row == 0)
        def _():
            gather_pages(order, pages_ref, buf, sem, 0, 0, count)

        @pl.when(row + 1 < rows)
        def _():
            gather_pages(order, pages_ref, buf, sem, row + 1, 1 - slot, count)

        q = q_ref[0].astype(f32)
        swapped = pltpu.roll(q, HALF, 1)
        own = (
            lax.broadcasted_iota(jnp.int32, (heads, width), 1) // HEAD_WIDTH
            == lax.broadcasted_iota(jnp.int32, (heads, width), 0) // group
        )
        wait_pages(pages_ref, buf, sem, slot, count)
        for m in range(turns):
            turned = q * t_ref[0, m][None] + swapped * t_ref[1, m][None]
            spread = jnp.where(own, jnp.concatenate([turned] * kv_heads, axis=1), 0.0).astype(bf16)
            n = per_turn // PAGE
            k = buf[slot, m * n : (m + 1) * n].reshape(per_turn, width)
            s = lax.dot_general(spread, k, (((1,), (1,)), ((), ())), preferred_element_type=f32)
            o_ref[0, :, m * per_turn : (m + 1) * per_turn] = s.astype(bf16)

    return pl.pallas_call(
        kernel,
        out_shape=jax.ShapeDtypeStruct((rows, heads, per_row), bf16),
        grid_spec=pltpu.PrefetchScalarGridSpec(
            num_scalar_prefetch=1,
            grid=(rows,),
            in_specs=[
                pl.BlockSpec(memory_space=pl.ANY),
                pl.BlockSpec((1, heads, HEAD_WIDTH), lambda i, _: (i, 0, 0)),
                pl.BlockSpec(tables.shape, lambda i, _: (0, 0, 0)),
            ],
            out_specs=pl.BlockSpec((1, heads, per_row), lambda i, _: (i, 0, 0)),
            scratch_shapes=[
                pltpu.VMEM((2, count, PAGE, width), bf16),
                pltpu.SemaphoreType.DMA((2,)),
            ],
        ),
        name="partial_scores",
    )(order, pages, queries, tables)


def sorted_states(order, states, rows):
    tokens, features = states.shape
    per_row = tokens // rows
    count = per_row // PAGE
    pages = states.reshape(tokens // PAGE, PAGE, features)

    def kernel(order, pages_ref, o_ref, buf, sem):
        row = pl.program_id(0)
        slot = lax.rem(row, 2)

        @pl.when(row == 0)
        def _():
            gather_pages(order, pages_ref, buf, sem, 0, 0, count)

        @pl.when(row + 1 < rows)
        def _():
            gather_pages(order, pages_ref, buf, sem, row + 1, 1 - slot, count)

        wait_pages(pages_ref, buf, sem, slot, count)
        o_ref[0] = buf[slot].reshape(per_row, features)

    return pl.pallas_call(
        kernel,
        out_shape=jax.ShapeDtypeStruct((rows, per_row, features), bf16),
        grid_spec=pltpu.PrefetchScalarGridSpec(
            num_scalar_prefetch=1,
            grid=(rows,),
            in_specs=[pl.BlockSpec(memory_space=pl.ANY)],
            out_specs=pl.BlockSpec((1, per_row, features), lambda i, _: (i, 0, 0)),
            scratch_shapes=[
                pltpu.VMEM((2, count, PAGE, features), bf16),
                pltpu.SemaphoreType.DMA((2,)),
            ],
        ),
        name="sorted_states",
    )(order, pages)


def fresh_weights(pieces):
    devices, heads, length = pieces.shape

    def kernel(p_ref, w_ref, s_ref):
        scores = p_ref[0].astype(f32)
        for d in range(1, devices):
            scores = scores + p_ref[d].astype(f32)
        peak = jnp.max(scores, axis=-1, keepdims=True)
        weights = jnp.exp(scores - peak).astype(bf16)
        total = jnp.sum(weights.astype(f32), axis=-1, keepdims=True)
        for d in range(devices):
            w_ref[d] = weights
        lane = lax.broadcasted_iota(jnp.int32, (heads, HEAD_WIDTH), 1)
        head = lax.broadcasted_iota(jnp.int32, (heads, HEAD_WIDTH), 0)
        spread = jnp.where(lane == head, peak, 0.0) + jnp.where(lane == head + heads, total, 0.0)
        s_ref[...] = jnp.broadcast_to(jnp.sum(spread, axis=0, keepdims=True), s_ref.shape)

    return pl.pallas_call(
        kernel,
        out_shape=(
            jax.ShapeDtypeStruct(pieces.shape, bf16),
            jax.ShapeDtypeStruct((8, HEAD_WIDTH), f32),
        ),
        name="fresh_weights",
    )(pieces)


def partial_outputs(weights, states, value_weight, stats, receivers):
    rows, heads, per_row = weights.shape
    features, width = value_weight.shape
    kv_heads = width // HEAD_WIDTH
    group = heads // kv_heads
    local = heads // receivers
    per_kv = group // local

    def kernel(w_ref, x_ref, v_ref, s_ref, o_ref, held, out, lanes):
        row = pl.program_id(0)
        y = jnp.dot(w_ref[0], x_ref[0], preferred_element_type=f32)
        at = pl.multiple_of(row * group, group)
        for j in range(kv_heads):
            held[j, pl.ds(at, group), :] = y[j * group : (j + 1) * group]

        @pl.when(row == rows - 1)
        def _():
            o_ref[:, local * HEAD_WIDTH :] = jnp.broadcast_to(
                s_ref[0:1], (rows * receivers, HEAD_WIDTH)
            )
            for j in range(kv_heads):
                out[j] = jnp.dot(
                    held[j].astype(bf16),
                    v_ref[:, j * HEAD_WIDTH : (j + 1) * HEAD_WIDTH],
                    preferred_element_type=f32,
                )
                for e in range(per_kv):
                    for c in range(local):
                        lanes[c, pl.ds(j * per_kv + e, rows, stride=receivers), :] = out[
                            j, pl.ds(e * local + c, rows, stride=group), :
                        ]
            for c in range(local):
                o_ref[:, c * HEAD_WIDTH : (c + 1) * HEAD_WIDTH] = lanes[c]

    return pl.pallas_call(
        kernel,
        out_shape=jax.ShapeDtypeStruct((rows * receivers, (local + 1) * HEAD_WIDTH), f32),
        grid=(rows,),
        in_specs=[
            pl.BlockSpec((1, heads, per_row), lambda i: (i, 0, 0)),
            pl.BlockSpec((1, per_row, features), lambda i: (i, 0, 0)),
            pl.BlockSpec((features, width), lambda i: (0, 0)),
            pl.BlockSpec((8, HEAD_WIDTH), lambda i: (0, 0)),
        ],
        out_specs=pl.BlockSpec((rows * receivers, (local + 1) * HEAD_WIDTH), lambda i: (0, 0)),
        scratch_shapes=[
            pltpu.VMEM((kv_heads, rows * group, features), f32),
            pltpu.VMEM((kv_heads, rows * group, HEAD_WIDTH), f32),
            pltpu.VMEM((local, rows * receivers, HEAD_WIDTH), f32),
        ],
        name="partial_outputs",
    )(weights, states, value_weight, stats)


def per_device(
    prefill_states,
    key_weight,
    value_weight,
    page_slot,
    decode_states,
    query_weight,
    cache_keys,
    cache_values,
    cached_length,
):
    tensor_size = lax.axis_size("tensor")
    group_size = lax.axis_size("group")
    tensor_rank = lax.axis_index("tensor")
    group_rank = lax.axis_index("group")
    decode_rows = decode_states.shape[0]
    tokens = prefill_states.shape[0]
    kv_width = key_weight.shape[1]
    kv_heads = kv_width // HEAD_WIDTH
    page_count = page_slot.shape[-1]
    per_owner = page_count // group_size
    block = page_count * PAGE
    fresh_per_row = block // decode_rows
    fresh_length = tensor_size * fresh_per_row
    senders_per_row = group_size // decode_rows
    from_sender = fresh_per_row // senders_per_row
    inv_scale = 1.0 / HEAD_WIDTH**0.5

    local_queries = jnp.dot(decode_states, query_weight, preferred_element_type=f32)
    local_width = local_queries.shape[1]
    local_heads = local_width // HEAD_WIDTH
    sent = jnp.repeat(local_queries.astype(bf16), senders_per_row, axis=0)
    slots = jnp.pad(page_slot.reshape(1, page_count).astype(bf16), ((0, 0), (0, 128 - page_count)))
    sent = jnp.concatenate([sent, jnp.broadcast_to(slots, (group_size, 128))], axis=1)
    sent = jnp.broadcast_to(sent[:, None], (group_size, tensor_size, local_width + 128))
    sent = sent.reshape(group_size * tensor_size, local_width + 128)
    received = lax.all_to_all(sent, BOTH, 0, 0, tiled=True)

    first = (group_rank % senders_per_row) * from_sender - fresh_length
    place = (
        jnp.arange(tensor_size, dtype=jnp.int32)[:, None] * fresh_per_row
        + jnp.arange(PAGE, dtype=jnp.int32)[None, :]
        + first
    )
    angles = place[..., None].astype(f32) * FREQUENCY_PAIR
    keys = partial_keys(prefill_states, key_weight, jnp.cos(angles), jnp.sin(angles) * SIGN_PAIR)

    head_total = tensor_size * local_heads
    queries = received[:, :local_width].reshape(group_size, head_total, HEAD_WIDTH)
    slot_of = lax.dynamic_slice(
        received, (group_rank * tensor_size, local_width), (tensor_size, page_count)
    ).astype(jnp.int32)
    index = jnp.arange(page_count, dtype=jnp.int32)
    page_of = jnp.sum(
        jnp.where(slot_of[None] == index[:, None, None], index[None, None, :], 0), axis=-1
    )
    order = (page_of + jnp.arange(tensor_size, dtype=jnp.int32)[None] * page_count).reshape(-1)

    turn = np.arange(per_owner)[:, None] * PAGE * np.concatenate([FREQUENCY, FREQUENCY])[None]
    tables = np.stack([np.cos(turn), -np.sin(turn) * SIGN_PAIR]).astype(np.float32) * np.float32(
        inv_scale
    )
    scores = partial_scores(order, keys, queries, jnp.asarray(tables))
    half = head_total * group_size // tensor_size
    fresh_row = scores.shape[-1]
    pieces = lax.all_to_all(
        scores.reshape(tensor_size, half, fresh_row), "tensor", 0, 0, tiled=True
    )

    states = sorted_states(order, prefill_states, group_size)

    query_position = cached_length + fresh_length
    own_queries = (
        apply_rotary(
            local_queries.reshape(decode_rows, local_heads, HEAD_WIDTH), query_position[:, None]
        )
        .reshape(decode_rows, local_width)
        .astype(bf16)
    )
    own_queries = jnp.moveaxis(sent_to_all(own_queries, "tensor"), 0, 1)
    grouped = own_queries.reshape(decode_rows, kv_heads, head_total // kv_heads, HEAD_WIDTH)
    context_dev = cache_keys.shape[1]
    prior_keys = cache_keys.reshape(decode_rows, context_dev, kv_heads, HEAD_WIDTH)
    prior_values = cache_values.reshape(decode_rows, context_dev, kv_heads, HEAD_WIDTH)
    old_scores = (
        jnp.einsum("bhgd,blhd->bhgl", grouped, prior_keys, preferred_element_type=f32) * inv_scale
    )
    usable = (tensor_rank * context_dev + jnp.arange(context_dev, dtype=jnp.int32))[
        None, :
    ] < cached_length[:, None]
    old_scores = jnp.where(usable[:, None, None, :], old_scores, masked_score)
    row_peak = jnp.max(old_scores, axis=-1)
    old_weights = jnp.exp(old_scores - row_peak[..., None])
    row_total = jnp.sum(old_weights, axis=-1)
    weighted = jnp.einsum(
        "bhgl,blhd->bhgd", old_weights.astype(bf16), prior_values, preferred_element_type=f32
    )
    shape = (decode_rows, tensor_size, local_heads)
    weighted = weighted.reshape(*shape, HEAD_WIDTH)
    old = jnp.concatenate(
        [
            jnp.moveaxis(weighted, 1, 0).reshape(tensor_size, decode_rows * local_heads, HEAD_WIDTH),
            jnp.pad(
                jnp.stack(
                    [
                        jnp.moveaxis(a.reshape(shape), 1, 0).reshape(tensor_size, -1)
                        for a in (row_peak, row_total)
                    ],
                    axis=1,
                ),
                ((0, 0), (0, 0), (0, HEAD_WIDTH - decode_rows * local_heads)),
            ),
        ],
        axis=1,
    )
    old = lax.all_to_all(old, "tensor", 0, 0, tiled=True)

    weights, stats = fresh_weights(pieces)
    weights = lax.all_to_all(weights, "tensor", 0, 0, tiled=True)
    weights = weights.reshape(group_size, head_total, fresh_row)
    outputs = partial_outputs(weights, states, value_weight, stats, tensor_size)
    outputs = lax.all_to_all(outputs, BOTH, 0, 0, tiled=True)

    own = decode_rows * local_heads
    old_stats = old[:, own:, :own].reshape(tensor_size, 2, decode_rows, local_heads)
    old_peak = jnp.max(old_stats[:, 0], axis=0)
    factor = jnp.exp(old_stats[:, 0] - old_peak[None])
    old_total = jnp.sum(old_stats[:, 1] * factor, axis=0)
    old_sum = jnp.sum(
        old[:, :own].reshape(tensor_size, decode_rows, local_heads, HEAD_WIDTH)
        * factor[..., None],
        axis=0,
    )
    outputs = outputs.reshape(group_size, tensor_size, local_width + HEAD_WIDTH)
    fresh_sum = jnp.sum(outputs[:, :, :local_width], axis=1).reshape(
        decode_rows, senders_per_row, local_heads, HEAD_WIDTH
    )
    per_source = half // local_heads
    source = group_rank * (tensor_size // group_size) + tensor_rank // per_source
    head_at = local_width + (tensor_rank % per_source) * local_heads
    fresh_peak, fresh_total = (
        lax.dynamic_slice(outputs, (0, source, at), (group_size, 1, local_heads)).reshape(
            decode_rows, senders_per_row, local_heads
        )
        for at in (head_at, head_at + half)
    )
    peak = jnp.maximum(old_peak, jnp.max(fresh_peak, axis=1))
    fresh_factor = jnp.exp(fresh_peak - peak[:, None])
    old_factor = jnp.exp(old_peak - peak)
    total = old_total * old_factor + jnp.sum(fresh_total * fresh_factor, axis=1)
    summed = old_sum * old_factor[..., None] + jnp.sum(fresh_sum * fresh_factor[..., None], axis=1)
    return (summed / total[..., None]).reshape(decode_rows, local_width).astype(bf16)


def solution(mesh):
    placed = (
        P("group", "tensor"),
        P("tensor", None),
        P("tensor", None),
        P("group", "tensor", None),
        P("group", None),
        P(None, "tensor"),
        P("group", "tensor", None),
        P("group", "tensor", None),
        P("group"),
    )
    return jax.shard_map(
        per_device, mesh=mesh, in_specs=placed, out_specs=P("group", "tensor"), check_vma=False
    )
```

```python
import jax
import jax.numpy as jnp
import numpy as np
from jax import lax
from jax.experimental import pallas as pl
from jax.experimental.pallas import tpu as pltpu
from jax.sharding import PartitionSpec as P


HEAD_WIDTH = 128
PAGE = 8
BOTH = ("group", "tensor")

rope_theta = 500000.0
masked_score = -1e30

bf16 = jnp.bfloat16
f32 = jnp.float32

HALF = HEAD_WIDTH // 2
FREQUENCY = rope_theta ** (-2.0 * np.arange(HALF) / HEAD_WIDTH)
FREQUENCY_PAIR = np.concatenate([FREQUENCY, FREQUENCY]).astype(np.float32)
SIGN_PAIR = np.concatenate([-np.ones(HALF), np.ones(HALF)]).astype(np.float32)


def apply_rotary(vectors, positions):
    angles = positions[..., None].astype(f32) * FREQUENCY.astype(np.float32)
    cosine_part = jnp.cos(angles)
    sine_part = jnp.sin(angles)
    first_half = vectors[..., :HALF]
    second_half = vectors[..., HALF:]
    return jnp.concatenate(
        [
            first_half * cosine_part - second_half * sine_part,
            second_half * cosine_part + first_half * sine_part,
        ],
        axis=-1,
    )


SMALL = pltpu.CompilerParams(vmem_limit_bytes=32 * 1024 * 1024)


def in_hbm(x):
    return pltpu.with_memory_space_constraint(x, pltpu.HBM)


def exchanged(x, axis):
    return lax.all_to_all(x, axis, 0, 0, tiled=True)


def swap_halves(x):
    return pltpu.roll(x, HALF, x.ndim - 1)


def packed_queries(decode_states, query_weight, page_slot, groups, receivers):
    rows, features = decode_states.shape
    width = query_weight.shape[1]
    heads = width // HEAD_WIDTH
    pages = page_slot.shape[-1]
    steps = 8
    depth = features // steps
    per_row = groups // rows

    def kernel(d_ref, w_ref, s_ref, q_ref, o_ref):
        at = pl.program_id(0)
        part = jnp.dot(d_ref[...], w_ref[...], preferred_element_type=f32)

        @pl.when(at == 0)
        def _():
            q_ref[...] = part

        @pl.when(at > 0)
        def _():
            q_ref[...] += part

        @pl.when(at == steps - 1)
        def _():
            lane = lax.broadcasted_iota(jnp.int32, (pages, pages), 1)
            head = lax.broadcasted_iota(jnp.int32, (pages, pages), 0)
            slot = jnp.sum(jnp.where(lane == head, s_ref[0], 0).astype(f32), axis=1, keepdims=True)
            lanes = lax.broadcasted_iota(jnp.int32, (pages, HEAD_WIDTH), 1).astype(f32)
            page = lax.broadcasted_iota(jnp.int32, (pages, HEAD_WIDTH), 0).astype(f32)
            inverse = jnp.sum(jnp.where(slot == lanes, page, 0.0), axis=0, keepdims=True)
            index = lax.broadcasted_iota(jnp.int32, (8, HEAD_WIDTH), 0)
            for r in range(rows):
                tile = jnp.where(index == heads, inverse, 0.0)
                for c in range(heads):
                    own = q_ref[r : r + 1, c * HEAD_WIDTH : (c + 1) * HEAD_WIDTH]
                    tile = jnp.where(index == c, own, tile)
                n = per_row * receivers
                o_ref[r * n : (r + 1) * n] = jnp.broadcast_to(
                    tile.astype(bf16)[None], (n, 8, HEAD_WIDTH)
                )

    return pl.pallas_call(
        kernel,
        out_shape=(
            jax.ShapeDtypeStruct((rows, width), f32),
            jax.ShapeDtypeStruct((groups * receivers, 8, HEAD_WIDTH), bf16),
        ),
        grid=(steps,),
        in_specs=[
            pl.BlockSpec((rows, depth), lambda i: (0, i)),
            pl.BlockSpec((depth, width), lambda i: (i, 0)),
            pl.BlockSpec((1, 1, pages), lambda i: (0, 0, 0)),
        ],
        out_specs=(
            pl.BlockSpec((rows, width), lambda i: (0, 0)),
            pl.BlockSpec((groups * receivers, 8, HEAD_WIDTH), lambda i: (0, 0, 0)),
        ),
        compiler_params=SMALL,
        name="packed_queries",
    )(decode_states, in_hbm(query_weight), page_slot)


def partial_keys(states, weight, cosine, sine):
    tokens, features = states.shape
    blocks = cosine.shape[0]
    rows = tokens // blocks
    width = weight.shape[1]
    step = 2 * HEAD_WIDTH

    def kernel(x_ref, w_ref, c_ref, s_ref, o_ref, mixed):
        @pl.when(pl.program_id(0) == 0)
        def _():
            low = lax.broadcasted_iota(jnp.int32, (features, HEAD_WIDTH), 1) < HALF
            for at in range(0, width, step):
                one = w_ref[:, at : at + HEAD_WIDTH].astype(f32)
                two = w_ref[:, at + HEAD_WIDTH : at + step].astype(f32)
                mixed[:, at : at + HEAD_WIDTH] = jnp.where(low, one, swap_halves(two)).astype(bf16)
                mixed[:, at + HEAD_WIDTH : at + step] = jnp.where(
                    low, swap_halves(one), two
                ).astype(bf16)

        x = x_ref[...]
        c = c_ref[0][None]
        s = s_ref[0][None]
        for at in range(0, width, step):
            k = jnp.dot(x, mixed[:, at : at + step], preferred_element_type=f32)
            first = k[:, :HEAD_WIDTH].reshape(rows // PAGE, PAGE, HEAD_WIDTH)
            second = k[:, HEAD_WIDTH:].reshape(rows // PAGE, PAGE, HEAD_WIDTH)
            o_ref[:, at : at + HEAD_WIDTH] = (
                (first * c - second * s).reshape(rows, HEAD_WIDTH).astype(bf16)
            )
            o_ref[:, at + HEAD_WIDTH : at + step] = (
                (second * c + first * s).reshape(rows, HEAD_WIDTH).astype(bf16)
            )

    return pl.pallas_call(
        kernel,
        out_shape=pltpu.VMEM((tokens, width), bf16),
        grid=(blocks,),
        in_specs=[
            pl.BlockSpec((rows, features), lambda i: (i, 0)),
            pl.BlockSpec((features, width), lambda i: (0, 0)),
            pl.BlockSpec((1, PAGE, HEAD_WIDTH), lambda i: (i, 0, 0)),
            pl.BlockSpec((1, PAGE, HEAD_WIDTH), lambda i: (i, 0, 0)),
        ],
        out_specs=pl.BlockSpec((rows, width), lambda i: (i, 0)),
        scratch_shapes=[pltpu.VMEM((features, width), bf16)],
        compiler_params=SMALL,
        name="partial_keys",
    )(states, weight, cosine, sine)


def start_pages(order, pages_ref, buf, sem, row, turns, blocks, only=None):
    per_block = order.shape[1]
    for m in range(turns) if only is None else (only,):
        for t in range(blocks):
            page = order[t, row * turns + m] + t * per_block
            pltpu.make_async_copy(pages_ref.at[page], buf.at[m * blocks + t], sem).start()


def wait_pages(pages_ref, buf, sem):
    pltpu.make_async_copy(pages_ref.at[pl.ds(0, buf.shape[0])], buf, sem).wait()


def partial_scores(order, keys, received, own_queries, tables, rows):
    tokens, width = keys.shape
    blocks, page_count = order.shape
    senders = received.shape[0] // rows
    local = own_queries.shape[1] // HEAD_WIDTH
    own_rows = own_queries.shape[0]
    heads = senders * local
    per_row = tokens // rows
    turns = tables.shape[1]
    per_turn = per_row // turns
    kv_heads = width // HEAD_WIDTH
    group = heads // kv_heads
    half = heads // 2
    pages = keys.reshape(tokens // PAGE, PAGE, width)

    def kernel(order, k_ref, r_ref, own_ref, t_ref, o_ref, line, chosen):
        row = pl.program_id(0)
        for m in range(turns):
            for t in range(blocks):
                page = order[t, row * turns + m] + t * page_count
                chosen[m * blocks + t] = k_ref[page]
        pair = lax.broadcasted_iota(jnp.int32, (heads, width), 1)
        head = lax.broadcasted_iota(jnp.int32, (heads, width), 0) // group
        mask = (pair // (2 * HEAD_WIDTH) == head // 2) & (
            lax.rem(pair, HEAD_WIDTH) // HALF == lax.rem(head, 2)
        )
        low = lax.broadcasted_iota(jnp.int32, (heads, HEAD_WIDTH), 1) < HALF
        for c in range(local):
            line[pl.ds(c, senders, stride=local), :] = r_ref[:, c, :].astype(f32)
        q = line[...]
        other = swap_halves(q)
        first = jnp.where(low, q, other)
        second = jnp.where(low, other, q)
        for m in range(turns):
            one = first * t_ref[0, m][None] + second * t_ref[1, m][None]
            two = second * t_ref[0, m][None] - first * t_ref[1, m][None]
            spread = jnp.where(
                mask, jnp.concatenate([one, two] * (kv_heads // 2), axis=1), 0.0
            ).astype(bf16)
            k = chosen[m * blocks : (m + 1) * blocks].reshape(per_turn, width)
            s = lax.dot_general(
                spread, k, (((1,), (1,)), ((), ())), preferred_element_type=f32
            ).astype(bf16)
            for e in range(2):
                o_ref[e, :half, m * per_turn : (m + 1) * per_turn] = s[e * half : (e + 1) * half]
        for e in range(2):
            o_ref[e, half:, :] = own_ref[...]

    own = jnp.pad(own_queries, ((0, 8 - own_rows), (0, 0)))
    return pl.pallas_call(
        kernel,
        out_shape=jax.ShapeDtypeStruct((rows * 2, half + 8, per_row), bf16),
        grid_spec=pltpu.PrefetchScalarGridSpec(
            num_scalar_prefetch=1,
            grid=(rows,),
            in_specs=[
                pl.BlockSpec(memory_space=pltpu.VMEM),
                pl.BlockSpec((senders, 8, HEAD_WIDTH), lambda i, _: (i, 0, 0)),
                pl.BlockSpec(own.shape, lambda i, _: (0, 0)),
                pl.BlockSpec(tables.shape, lambda i, _: (0, 0, 0)),
            ],
            out_specs=pl.BlockSpec((2, half + 8, per_row), lambda i, _: (i, 0, 0)),
            scratch_shapes=[
                pltpu.VMEM((heads, HEAD_WIDTH), f32),
                pltpu.VMEM((turns * blocks, PAGE, width), bf16),
            ],
        ),
        compiler_params=SMALL,
        name="partial_scores",
    )(order, pages, received, own, tables)


def sorted_states(order, states, rows, turns):
    tokens, features = states.shape
    blocks = order.shape[0]
    per_row = tokens // rows
    count = per_row // PAGE
    pages = in_hbm(states.reshape(tokens // PAGE, PAGE, features))

    def kernel(order, pages_ref, o_ref, buf, sem):
        row = pl.program_id(0)
        slot = lax.rem(row, 2)

        @pl.when(row == 0)
        def _():
            start_pages(order, pages_ref, buf.at[0], sem.at[0], 0, turns, blocks)

        @pl.when(row + 1 < rows)
        def _():
            start_pages(order, pages_ref, buf.at[1 - slot], sem.at[1 - slot], row + 1, turns, blocks)

        wait_pages(pages_ref, buf.at[slot], sem.at[slot])
        o_ref[0] = buf[slot].reshape(per_row, features)

    return pl.pallas_call(
        kernel,
        out_shape=pltpu.HBM((rows, per_row, features), bf16),
        grid_spec=pltpu.PrefetchScalarGridSpec(
            num_scalar_prefetch=1,
            grid=(rows,),
            in_specs=[pl.BlockSpec(memory_space=pl.ANY)],
            out_specs=pl.BlockSpec((1, per_row, features), lambda i, _: (i, 0, 0)),
            scratch_shapes=[
                pltpu.VMEM((2, count, PAGE, features), bf16),
                pltpu.SemaphoreType.DMA((2,)),
            ],
        ),
        compiler_params=SMALL,
        name="sorted_states",
    )(order, pages)


def thirds(x):
    high = x.astype(bf16).astype(f32)
    rest = x - high
    middle = rest.astype(bf16).astype(f32)
    return high, middle, (rest - middle).astype(bf16).astype(f32)


def fresh_weights(pieces, heads):
    devices, _, length = pieces.shape

    def kernel(p_ref, w_ref, s_ref):
        scores = p_ref[0, :heads].astype(f32)
        for d in range(1, devices):
            scores = scores + p_ref[d, :heads].astype(f32)
        peak = jnp.max(scores, axis=-1, keepdims=True)
        weights = jnp.exp(scores - peak).astype(bf16)
        total = jnp.sum(weights.astype(f32), axis=-1, keepdims=True)
        for d in range(devices):
            w_ref[d] = weights
        lane = lax.broadcasted_iota(jnp.int32, (heads, HEAD_WIDTH), 1)
        head = lax.broadcasted_iota(jnp.int32, (heads, HEAD_WIDTH), 0)
        index = lax.broadcasted_iota(jnp.int32, (8, HEAD_WIDTH), 0)
        tile = jnp.zeros((8, HEAD_WIDTH), f32)
        for at, stat in ((4, peak), (5, total)):
            spread = jnp.zeros((heads, HEAD_WIDTH), f32)
            for n, part in enumerate(thirds(stat)):
                spread = jnp.where(lane == head + n * heads, part, spread)
            tile = jnp.where(index == at, jnp.sum(spread, axis=0, keepdims=True), tile)
        s_ref[...] = tile

    return pl.pallas_call(
        kernel,
        out_shape=(
            jax.ShapeDtypeStruct((devices, heads, length), bf16),
            jax.ShapeDtypeStruct((8, HEAD_WIDTH), f32),
        ),
        compiler_params=SMALL,
        name="fresh_weights",
    )(pieces)


def partial_outputs(weights, states, value_weight, stats, receivers):
    rows, heads, per_row = weights.shape
    features, width = value_weight.shape
    kv_heads = width // HEAD_WIDTH
    group = heads // kv_heads
    local = heads // receivers
    per_kv = group // local

    def kernel(w_ref, x_ref, v_ref, s_ref, o_ref, held):
        row = pl.program_id(0)
        y = jnp.dot(w_ref[0], x_ref[0], preferred_element_type=f32)
        at = pl.multiple_of(row * group, group)
        for j in range(kv_heads):
            held[j, pl.ds(at, group), :] = y[j * group : (j + 1) * group]

        @pl.when(row == rows - 1)
        def _():
            stat = s_ref[...]
            top = lax.broadcasted_iota(jnp.int32, (8, HEAD_WIDTH), 0) < local
            for j in range(kv_heads):
                out = jnp.dot(
                    held[j].astype(bf16),
                    v_ref[:, j * HEAD_WIDTH : (j + 1) * HEAD_WIDTH],
                    preferred_element_type=f32,
                )
                for o in range(rows):
                    tile = out[o * group : (o + 1) * group]
                    for e in range(per_kv):
                        moved = tile if e == 0 else pltpu.roll(tile, group - e * local, 0)
                        o_ref[o * receivers + j * per_kv + e] = jnp.where(top, moved, stat).astype(
                            bf16
                        )

    return pl.pallas_call(
        kernel,
        out_shape=jax.ShapeDtypeStruct((rows * receivers, 8, HEAD_WIDTH), bf16),
        grid=(rows,),
        in_specs=[
            pl.BlockSpec((1, heads, per_row), lambda i: (i, 0, 0)),
            pl.BlockSpec((1, per_row, features), lambda i: (i, 0, 0)),
            pl.BlockSpec((features, width), lambda i: (0, 0)),
            pl.BlockSpec((8, HEAD_WIDTH), lambda i: (0, 0)),
        ],
        out_specs=pl.BlockSpec((rows * receivers, 8, HEAD_WIDTH), lambda i: (0, 0, 0)),
        scratch_shapes=[pltpu.VMEM((kv_heads, rows * group, features), f32)],
        compiler_params=SMALL,
        name="partial_outputs",
    )(weights, in_hbm(states), value_weight, stats)


def cache_attention(pieces, keys, values, limits, start):
    senders, high, length = pieces.shape
    rows, context, width = keys.shape
    local = length // HEAD_WIDTH
    heads = senders * local
    kv_heads = width // HEAD_WIDTH
    group = heads // kv_heads
    per_kv = group // local

    def kernel(limit, first, p_ref, k_ref, v_ref, o_ref, line):
        row = pl.program_id(0)

        @pl.when(row == 0)
        def _():
            for b in range(rows):
                for c in range(local):
                    line[b, pl.ds(c, senders, stride=local), :] = p_ref[
                        :, b, c * HEAD_WIDTH : (c + 1) * HEAD_WIDTH
                    ].astype(f32)

        own = (
            lax.broadcasted_iota(jnp.int32, (heads, width), 1) // HEAD_WIDTH
            == lax.broadcasted_iota(jnp.int32, (heads, width), 0) // group
        )
        q = line[row]
        spread = jnp.where(own, jnp.concatenate([q] * kv_heads, axis=1), 0.0).astype(bf16)
        scores = lax.dot_general(
            spread, k_ref[0], (((1,), (1,)), ((), ())), preferred_element_type=f32
        ) * (1.0 / HEAD_WIDTH**0.5)
        place = lax.broadcasted_iota(jnp.int32, (heads, context), 1) + first[0]
        scores = jnp.where(place < limit[row], scores, masked_score)
        peak = jnp.max(scores, axis=-1, keepdims=True)
        weights = jnp.exp(scores - peak)
        total = jnp.sum(weights, axis=-1, keepdims=True)
        low = lax.broadcasted_iota(jnp.int32, (heads, HEAD_WIDTH), 1) < HALF
        stats = jnp.where(low, peak, total)
        sums = jnp.dot(weights.astype(bf16), v_ref[0], preferred_element_type=f32)
        top = lax.broadcasted_iota(jnp.int32, (group, HEAD_WIDTH), 0) < local
        for j in range(kv_heads):
            tile = sums[j * group : (j + 1) * group, j * HEAD_WIDTH : (j + 1) * HEAD_WIDTH]
            stat = stats[j * group : (j + 1) * group]
            o_ref[j * per_kv, 0] = jnp.where(top, tile, pltpu.roll(stat, local, 0))
            o_ref[j * per_kv + 1, 0] = jnp.where(top, pltpu.roll(tile, local, 0), stat)

    return pl.pallas_call(
        kernel,
        out_shape=jax.ShapeDtypeStruct((senders, rows, group, HEAD_WIDTH), f32),
        grid_spec=pltpu.PrefetchScalarGridSpec(
            num_scalar_prefetch=2,
            grid=(rows,),
            in_specs=[
                pl.BlockSpec((senders, 8, length), lambda i, *_: (0, high // 8 - 1, 0)),
                pl.BlockSpec((1, context, width), lambda i, *_: (i, 0, 0)),
                pl.BlockSpec((1, context, width), lambda i, *_: (i, 0, 0)),
            ],
            out_specs=pl.BlockSpec((senders, 1, group, HEAD_WIDTH), lambda i, *_: (0, i, 0, 0)),
            scratch_shapes=[pltpu.VMEM((rows, heads, HEAD_WIDTH), f32)],
        ),
        compiler_params=SMALL,
        name="cache_attention",
    )(limits, start, pieces, in_hbm(keys), in_hbm(values))


def joined(old, fresh, source, head_at, half, senders):
    devices, rows, group, _ = old.shape
    local = group // 2

    def kernel(source, head_at, old_ref, fresh_ref, o_ref):
        low = lax.broadcasted_iota(jnp.int32, (group, HEAD_WIDTH), 1) < HALF
        lane = lax.broadcasted_iota(jnp.int32, (group, HEAD_WIDTH), 1)
        index = lax.broadcasted_iota(jnp.int32, (group, HEAD_WIDTH), 0)
        chosen = (
            (lax.rem(lane, half) == head_at[0] + index) & (lane < 3 * half) & (index < local)
        )
        for b in range(rows):
            parts = []
            for d in range(devices):
                tile = old_ref[d, b]
                stat = pltpu.roll(tile, local, 0)
                other = swap_halves(stat)
                parts.append((jnp.where(low, stat, other), jnp.where(low, other, stat), tile))
            for n in range(senders):
                at = (b * senders + n) * devices
                tile = fresh_ref[at].astype(f32)
                for d in range(1, devices):
                    tile = tile + fresh_ref[at + d].astype(f32)
                stat = fresh_ref[at + source[0]].astype(f32)
                peak, total = (
                    jnp.sum(
                        jnp.where(chosen, stat[local + k : local + k + 1], 0.0),
                        axis=1,
                        keepdims=True,
                    )
                    for k in range(2)
                )
                parts.append(
                    (
                        jnp.broadcast_to(peak, tile.shape),
                        jnp.broadcast_to(total, tile.shape),
                        tile,
                    )
                )
            top = parts[0][0]
            for peak, _, _ in parts[1:]:
                top = jnp.maximum(top, peak)
            total = jnp.zeros_like(top)
            value = jnp.zeros_like(top)
            for peak, part, tile in parts:
                factor = jnp.exp(peak - top)
                total = total + part * factor
                value = value + tile * factor
            result = value / total
            for c in range(local):
                o_ref[b : b + 1, c * HEAD_WIDTH : (c + 1) * HEAD_WIDTH] = result[c : c + 1]

    return pl.pallas_call(
        kernel,
        out_shape=jax.ShapeDtypeStruct((rows, local * HEAD_WIDTH), f32),
        in_specs=[
            pl.BlockSpec(memory_space=pltpu.SMEM),
            pl.BlockSpec(memory_space=pltpu.SMEM),
            pl.BlockSpec(memory_space=pltpu.VMEM),
            pl.BlockSpec(memory_space=pltpu.VMEM),
        ],
        compiler_params=SMALL,
        name="joined",
    )(source, head_at, old, fresh)


def per_device(
    prefill_states,
    key_weight,
    value_weight,
    page_slot,
    decode_states,
    query_weight,
    cache_keys,
    cache_values,
    cached_length,
):
    tensor_size = lax.axis_size("tensor")
    group_size = lax.axis_size("group")
    tensor_rank = lax.axis_index("tensor")
    group_rank = lax.axis_index("group")
    decode_rows = decode_states.shape[0]
    page_count = page_slot.shape[-1]
    per_owner = page_count // group_size
    block = page_count * PAGE
    fresh_per_row = block // decode_rows
    fresh_length = tensor_size * fresh_per_row
    senders_per_row = group_size // decode_rows
    from_sender = fresh_per_row // senders_per_row
    inv_scale = 1.0 / HEAD_WIDTH**0.5

    local_queries, sent = packed_queries(
        decode_states, query_weight, page_slot, group_size, tensor_size
    )
    local_width = local_queries.shape[1]
    local_heads = local_width // HEAD_WIDTH
    received = exchanged(sent, BOTH)

    first = (group_rank % senders_per_row) * from_sender - fresh_length
    place = (
        jnp.arange(tensor_size, dtype=jnp.int32)[:, None] * fresh_per_row
        + jnp.arange(PAGE, dtype=jnp.int32)[None, :]
        + first
    )
    angles = place[..., None].astype(f32) * FREQUENCY_PAIR
    cosine, sine = jnp.cos(angles), jnp.sin(angles)
    query_position = cached_length + fresh_length
    own_queries = (
        apply_rotary(
            local_queries.reshape(decode_rows, local_heads, HEAD_WIDTH), query_position[:, None]
        )
        .reshape(decode_rows, local_width)
        .astype(bf16)
    )
    keys = partial_keys(in_hbm(prefill_states), key_weight, cosine, sine)

    head_total = tensor_size * local_heads
    order = lax.dynamic_slice(
        received, (group_rank * tensor_size, local_heads, 0), (tensor_size, 1, page_count)
    )
    order = order.reshape(tensor_size, page_count).astype(jnp.int32)
    turn = np.arange(per_owner)[:, None] * PAGE * np.concatenate([FREQUENCY, FREQUENCY])[None]
    tables = (np.stack([np.cos(turn), np.sin(turn)]) * inv_scale).astype(np.float32)
    scores = partial_scores(order, keys, received, own_queries, jnp.asarray(tables), group_size)
    half = head_total * group_size // tensor_size
    fresh_row = scores.shape[-1]
    pieces = exchanged(scores, "tensor")

    states = sorted_states(order, prefill_states, group_size, per_owner)

    weights, stats = fresh_weights(pieces, half)
    weights = exchanged(weights, "tensor")

    context_dev = cache_keys.shape[1]
    start = (tensor_rank * context_dev).astype(jnp.int32).reshape(1)
    old = cache_attention(pieces, cache_keys, cache_values, cached_length, start)
    old = exchanged(old, "tensor")

    weights = weights.reshape(group_size, head_total, fresh_row)
    outputs = partial_outputs(weights, states, value_weight, stats, tensor_size)
    outputs = exchanged(outputs, BOTH)

    per_source = half // local_heads
    source = group_rank * (tensor_size // group_size) + tensor_rank // per_source
    head_at = (tensor_rank % per_source) * local_heads
    result = joined(
        old,
        outputs,
        source.astype(jnp.int32).reshape(1),
        head_at.astype(jnp.int32).reshape(1),
        half,
        senders_per_row,
    )
    return result.astype(bf16)


def solution(mesh):
    placed = (
        P("group", "tensor"),
        P("tensor", None),
        P("tensor", None),
        P("group", "tensor", None),
        P("group", None),
        P(None, "tensor"),
        P("group", "tensor", None),
        P("group", "tensor", None),
        P("group"),
    )

    return jax.shard_map(
        per_device, mesh=mesh, in_specs=placed, out_specs=P("group", "tensor"), check_vma=False
    )
```
